32 devices in a mesh: rep: 4 (over y, x), exp: 8 (over z, core).
Axes of the slice: x: 2, y: 2, z: 4, core: 2. Of those that a mesh axis runs over, the one named last changes fastest.
Arguments:
- tokens: bfloat16 [4096, 1024], P(('rep', 'exp')), may hold values from -6 to 6
- gain: float32 [1024], replicated, may hold values from 0.1 to 1.9
- expert_ids: int32 [4096, 2], P(('rep', 'exp')), may hold values from 0 to 7, all different within a row
- gates: float32 [4096, 2], P(('rep', 'exp')), may hold values from 0.1 to 0.9
- w_in: bfloat16 [8, 1024, 4096], P('exp', None, 'rep'), may hold values from -0.1875 to 0.1875
- w_out: bfloat16 [8, 4096, 1024], P('exp', 'rep'), may hold values from -0.09375 to 0.09375
- cotangent: bfloat16 [4096, 1024], P(('rep', 'exp')), may hold values from -6 to 6
Outputs:
- mixed: bfloat16 [4096, 1024], P(('rep', 'exp'))
- grad_tokens: bfloat16 [4096, 1024], P(('rep', 'exp'))
- grad_in: bfloat16 [8, 1024, 4096], P('exp', None, 'rep')
- grad_out: bfloat16 [8, 4096, 1024], P('exp', 'rep')
The draws below stay inside these ranges and needn't reach their ends.
Inputs may be any that keep to these rules, and one draw needn't show every extreme that they name: `expert_ids`: each token names two different experts, and every expert is named by some token.
All inputs are finite; a program needn't handle non-finite values.
Results may differ from the reference program's by a relative error of at most 0.007.
Values may be sent and summed in bfloat16 or wider, within the bound.
No kernel may reach another device: no remote copies, remote signals or barrier semaphores. Data moves between devices by JAX's collectives and lax.ppermute only.
A program may use at most 64 MiB of HBM per device.

```python
import jax
import jax.numpy as jnp
from jax import lax

D = 1024
FF = 4096
TOK_DEV = 128
EXPERTS = 8
CAP = 32
TOKENS = 4096
N_REP = 4


def levels(key, shape, cuts, low, top_value):
    def one(axis_at, parts):
        draws = jax.random.uniform(jax.random.fold_in(jax.random.fold_in(key, 6), axis_at), (parts,), jnp.float32, low / len(cuts), top_value / len(cuts))
        return jnp.repeat(jnp.exp(draws), shape[axis_at] // parts).reshape((-1,) + (1,) * (len(shape) - axis_at - 1))

    loudness = one(*cuts[0])
    for cut in cuts[1:]:
        loudness = loudness * one(*cut)
    return loudness


def distinct(stream_key, rows, amount, top, lift):
    order = jax.random.permutation(jax.random.fold_in(stream_key, 1), amount)
    boost = order
    for power in range(3):
        boost = boost * boost // amount
    boost = boost * lift // amount
    tickets = jax.random.randint(jax.random.fold_in(stream_key, 2), (rows, amount), 0, 4096) + boost
    holders = jax.random.permutation(jax.random.fold_in(stream_key, 3), rows)[jnp.arange(amount) % rows]
    tickets = jnp.where(jnp.arange(rows)[:, None] == holders[None, :], 1 << 14, tickets)
    priority = tickets * amount + jnp.arange(amount)
    return lax.top_k(priority.astype(jnp.int32), top)[1].astype(jnp.int32)


def centred(own_key, shape, deviation, most, shards=(), kind=jnp.bfloat16):
    loudness = levels(own_key, shape, shards, -0.22, 0.18) if shards else 1.0
    array = jax.random.normal(own_key, shape, jnp.float32) * deviation * loudness
    return jnp.minimum(jnp.maximum(array, -most), most).astype(kind)


def setup_inputs(seed: int = 0) -> dict:
    streams_of = jax.random.split(jax.random.key(seed), 8)
    return {
        "tokens": centred(streams_of[0], (TOKENS, D), 1.0, 6.0, ((0, 32),)),
        "gain": jnp.clip(1.0 + 0.18 * jax.random.normal(streams_of[1], (D,), jnp.float32), 0.1, 1.9),
        "expert_ids": distinct(streams_of[2], TOKENS, EXPERTS, 2, 2048),
        "gates": jnp.clip(0.1 + 0.79999997 * jax.random.uniform(streams_of[3], (TOKENS, 2), jnp.float32) ** levels(streams_of[3], (TOKENS, 2), ((0, 32),), -0.2, 0.2), 0.1, 0.9),
        "w_in": centred(streams_of[4], (EXPERTS, D, FF), D ** -0.5, 0.1875, ((0, 8), (2, 4))),
        "w_out": centred(streams_of[5], (EXPERTS, FF, D), FF ** -0.5, 0.09375, ((0, 8), (1, 4))),
        "cotangent": centred(streams_of[6], (TOKENS, D), 1.0, 6.0, ((0, 32),)),
    }


epsilon = 1e-05

def normalize(entries, gain):
    center = entries - lax.optimization_barrier(jnp.mean(entries, axis=-1, keepdims=True))
    spread = lax.optimization_barrier(jnp.mean(center * center, axis=-1, keepdims=True))
    return center * lax.rsqrt(spread + epsilon) * gain

def activate(entries):
    return jax.nn.gelu(entries, approximate=True)

def grouped_second(hidden, w_second):
    width = FF // N_REP
    total = jnp.zeros((hidden.shape[0], w_second.shape[1]), jnp.float32)
    for group in range(N_REP):
        piece = jnp.dot(hidden[:, group * width:(group + 1) * width], w_second[group * width:(group + 1) * width], preferred_element_type=jnp.float32)
        total = total + piece.astype(jnp.bfloat16).astype(jnp.float32)
    return total.astype(jnp.bfloat16)

def grouped_first(d_pre, w_first):
    width = FF // N_REP
    total = jnp.zeros((d_pre.shape[0], w_first.shape[0]), jnp.float32)
    for group in range(N_REP):
        piece = jnp.dot(d_pre[:, group * width:(group + 1) * width], w_first[:, group * width:(group + 1) * width].T, preferred_element_type=jnp.float32)
        total = total + piece.astype(jnp.bfloat16).astype(jnp.float32)
    return total.astype(jnp.bfloat16)

def per_expert(operands):
    in_rows, grad_rows, w_first, w_second = operands
    preact = jnp.dot(in_rows, w_first, preferred_element_type=jnp.float32)
    activated, act_back = jax.vjp(activate, preact)
    hidden = activated.astype(jnp.bfloat16)
    out_rows = grouped_second(hidden, w_second)
    d_hidden = jnp.dot(grad_rows, w_second.T, preferred_element_type=jnp.float32)
    d_pre = act_back(d_hidden)[0].astype(jnp.bfloat16)
    grad_second = jnp.dot(hidden.T, grad_rows, preferred_element_type=jnp.float32).astype(jnp.bfloat16)
    grad_first = jnp.dot(in_rows.T, d_pre, preferred_element_type=jnp.float32).astype(jnp.bfloat16)
    d_rows = grouped_first(d_pre, w_first)
    return (out_rows, d_rows, grad_first, grad_second)

def reference(tokens, gain, expert_ids, gates, w_in, w_out, cotangent):
    blocks = TOKENS // TOK_DEV
    slots_all = blocks * CAP
    values = tokens.astype(jnp.float32)
    normed, norm_back = jax.vjp(lambda entries: normalize(entries, gain), values)
    normed = normed.astype(jnp.bfloat16)
    chosen = expert_ids.reshape(blocks, 2 * TOK_DEV)
    labels = jnp.arange(EXPERTS, dtype=jnp.int32)
    onehot = (chosen[:, :, None] == labels[None, None, :]).astype(jnp.int32)
    before = jnp.cumsum(onehot, axis=1) - onehot
    ranking = lax.optimization_barrier(jnp.sum(before * onehot, axis=2))
    kept_mask = ranking < CAP
    anchor = jnp.arange(blocks, dtype=jnp.int32)[:, None] * CAP
    slot_row = jnp.where(kept_mask, anchor + ranking, slots_all).reshape(-1).astype(jnp.int32)
    owners = chosen.reshape(-1).astype(jnp.int32)
    paired = jnp.repeat(normed, 2, axis=0)
    scaled = (cotangent.astype(jnp.float32)[:, None, :] * gates[:, :, None]).astype(jnp.bfloat16)
    scaled = scaled.reshape(2 * TOKENS, D)
    blank_rows = jnp.zeros((EXPERTS, slots_all + 1, D), jnp.bfloat16)
    expert_in = blank_rows.at[owners, slot_row].set(paired)[:, :slots_all]
    d_out = blank_rows.at[owners, slot_row].set(scaled)[:, :slots_all]
    out_rows, d_rows, grad_in, grad_out = lax.map(per_expert, (expert_in, d_out, w_in, w_out))
    zero_row = jnp.zeros((EXPERTS, 1, D), jnp.bfloat16)
    out_padded = jnp.concatenate([out_rows, zero_row], axis=1)
    returned = out_padded[owners, slot_row].astype(jnp.float32).reshape(TOKENS, 2, D)
    mixed = (values + lax.optimization_barrier(jnp.sum(gates[:, :, None] * returned, axis=1))).astype(jnp.bfloat16)
    d_padded = jnp.concatenate([d_rows, zero_row], axis=1)
    d_normed = lax.optimization_barrier(jnp.sum(d_padded[owners, slot_row].astype(jnp.float32).reshape(TOKENS, 2, D), axis=1))
    grad_tokens = (cotangent.astype(jnp.float32) + norm_back(d_normed)[0]).astype(jnp.bfloat16)
    return (mixed, grad_tokens, grad_in, grad_out)
```

```python
import jax
import jax.numpy as jnp
from jax import lax
from jax.sharding import PartitionSpec as P

epsilon = 1e-05


def chunks_of(chips):
    if chips == 4:
        return ((0,), (1, 3), (2,))
    return ((0,), tuple(range(1, chips // 2)), tuple(range(chips // 2, chips)))


def normalize(entries, gain):
    center = entries - jnp.mean(entries, axis=-1, keepdims=True)
    spread = jnp.mean(center * center, axis=-1, keepdims=True)
    return center * lax.rsqrt(spread + epsilon) * gain


def activate(entries):
    return jax.nn.gelu(entries, approximate=True)


def slot_table(labels_of, places_count, capacity):
    flattened = labels_of.reshape(-1)
    labels = jnp.arange(places_count // capacity, dtype=jnp.int32)
    onehot = (flattened[:, None] == labels[None, :]).astype(jnp.int32)
    before = jnp.cumsum(onehot, axis=0) - onehot
    ranking = jnp.sum(before * onehot, axis=1)
    target = jnp.where(ranking < capacity, flattened * capacity + ranking, -1)
    places = jnp.arange(places_count, dtype=jnp.int32)
    return (target[None, :] == places[:, None]).astype(jnp.bfloat16)


def take_rows(select, landed):
    return jnp.einsum("sp,sd->pd", select, landed, preferred_element_type=jnp.float32)


def flip(array, axis_name, mask):
    size = lax.axis_size(axis_name)
    return lax.ppermute(array, axis_name, [(i, i ^ mask) for i in range(size)])


def gather_rep(own, half):
    by_x = flip(own, "rep", 1)
    by_y = flip(own, "rep", 2)
    far_a = flip(by_y[:half], "rep", 1)
    far_b = flip(by_x[half:], "rep", 2)
    return jnp.concatenate([own, by_x, by_y, far_a, far_b], axis=0)


def f32(array):
    return array.astype(jnp.float32)


def scatter_rep(parts, half):
    p0, p1, p2, p3 = parts[0], parts[1], parts[2], parts[3]
    got_x = flip(jnp.concatenate([p1[:half], p3[:half]], axis=0), "rep", 1)
    got_y = flip(jnp.concatenate([p2[half:], p3[half:]], axis=0), "rep", 2)
    via_x = (f32(p2[:half]) + f32(got_x[half:])).astype(jnp.bfloat16)
    via_y = (f32(p1[half:]) + f32(got_y[half:])).astype(jnp.bfloat16)
    last_a = flip(via_x, "rep", 2)
    last_b = flip(via_y, "rep", 1)
    first = f32(p0[:half]) + f32(got_x[:half]) + f32(last_a)
    second = f32(p0[half:]) + f32(got_y[:half]) + f32(last_b)
    return jnp.concatenate([first, second], axis=0).astype(jnp.bfloat16)


def chunk_compute(rows, w_first, w_second, features):
    x_rows, d_rows = rows[:, :features], rows[:, features:]
    preact = jnp.dot(x_rows, w_first, preferred_element_type=jnp.float32)
    activated, act_back = jax.vjp(activate, preact)
    hidden = activated.astype(jnp.bfloat16)
    y_part = jnp.dot(hidden, w_second, preferred_element_type=jnp.float32)
    d_hidden = jnp.einsum("rd,fd->rf", d_rows, w_second, preferred_element_type=jnp.float32)
    d_pre = act_back(d_hidden)[0].astype(jnp.bfloat16)
    dx_part = jnp.einsum("rf,df->rd", d_pre, w_first, preferred_element_type=jnp.float32)
    parts = jnp.concatenate([y_part.astype(jnp.bfloat16), dx_part.astype(jnp.bfloat16)], axis=1)
    return hidden, d_pre, parts


def local(tokens, gain, expert_ids, gates, w_in, w_out, cotangent):
    experts = lax.axis_size("exp")
    chips = experts // 2
    tok_count, features = tokens.shape
    capacity = max(2, 2 * tok_count // experts)
    me = lax.axis_index("exp")
    values = tokens.astype(jnp.float32)
    normed, norm_back = jax.vjp(lambda entries: normalize(entries, gain), values)
    normed = normed.astype(jnp.bfloat16)
    select = slot_table(expert_ids ^ me, experts * capacity, capacity)
    scaled = (cotangent.astype(jnp.float32)[:, None, :] * gates[:, :, None]).astype(jnp.bfloat16)
    paired = jnp.concatenate(
        [jnp.repeat(normed, 2, axis=0), scaled.reshape(2 * tok_count, features)], axis=1
    )
    sent = jnp.dot(select, paired, preferred_element_type=jnp.float32).astype(jnp.bfloat16)
    sent = sent.reshape(chips, 2, capacity, 2 * features)
    swapped = flip(sent[:, 1], "exp", 1)
    outgoing = jnp.concatenate([sent[:, 0], swapped], axis=1)
    landed = [outgoing[0]] + [flip(outgoing[k], "exp", 2 * k) for k in range(1, chips)]
    w_first, w_second = w_in[0], w_out[0]
    rows_all, hidden_all, d_pre_all, parts_all = [], [], [], []
    chunks = chunks_of(chips)
    for chunk in chunks:
        own = jnp.concatenate([landed[k] for k in chunk], axis=0)
        count = own.shape[0]
        rows = gather_rep(own, count // 2)
        hidden, d_pre, parts = chunk_compute(rows, w_first, w_second, features)
        rows_all.append(rows)
        hidden_all.append(hidden)
        d_pre_all.append(d_pre)
        parts_all.append(parts.reshape(4, count, 2 * features))
    back = [None] * chips
    for at in (1, 2, 0):
        summed = scatter_rep(parts_all[at], parts_all[at].shape[1] // 2)
        for i, k in enumerate(chunks[at]):
            piece = summed[i * 2 * capacity : (i + 1) * 2 * capacity]
            back[k] = flip(piece, "exp", 2 * k) if k else piece
    rows_c = jnp.concatenate(rows_all, axis=0)
    hidden_c = jnp.concatenate(hidden_all, axis=0)
    d_pre_c = jnp.concatenate(d_pre_all, axis=0)
    grad_second = jnp.einsum(
        "rf,rd->fd", hidden_c, rows_c[:, features:], preferred_element_type=jnp.float32
    ).astype(jnp.bfloat16)
    grad_first = jnp.einsum(
        "rd,rf->df", rows_c[:, :features], d_pre_c, preferred_element_type=jnp.float32
    ).astype(jnp.bfloat16)
    stacked = jnp.stack(back)
    other = flip(stacked[:, capacity:], "exp", 1)
    returned = jnp.concatenate([stacked[:, :capacity], other], axis=1)
    returned = returned.reshape(experts * capacity, 2 * features)
    taken = take_rows(select, returned).reshape(tok_count, 2, 2 * features)
    mixed = (values + jnp.sum(gates[:, :, None] * taken[:, :, :features], axis=1)).astype(jnp.bfloat16)
    d_normed = jnp.sum(taken[:, :, features:], axis=1)
    grad_tokens = (cotangent.astype(jnp.float32) + norm_back(d_normed)[0]).astype(jnp.bfloat16)
    return (mixed, grad_tokens, grad_first[None], grad_second[None])


def solution(mesh):
    return jax.shard_map(
        local,
        mesh=mesh,
        in_specs=(
            P(("rep", "exp"), None),
            P(),
            P(("rep", "exp"), None),
            P(("rep", "exp"), None),
            P("exp", None, "rep"),
            P("exp", "rep", None),
            P(("rep", "exp"), None),
        ),
        out_specs=(
            P(("rep", "exp"), None),
            P(("rep", "exp"), None),
            P("exp", None, "rep"),
            P("exp", "rep", None),
        ),
        check_vma=False,
    )
```

```python
import functools

import jax
import jax.numpy as jnp
from jax import lax
from jax.experimental import pallas as pl
from jax.experimental.pallas import tpu as pltpu
from jax.sharding import PartitionSpec as P

epsilon = 1e-05
ROOT_2_PI = 0.7978845608028654
CUBIC = 0.044715
BF16, F32 = jnp.bfloat16, jnp.float32


def normalize(entries, gain):
    center = entries - jnp.mean(entries, axis=-1, keepdims=True)
    spread = jnp.mean(center * center, axis=-1, keepdims=True)
    return center * lax.rsqrt(spread + epsilon) * gain


def activate(entries):
    return jax.nn.gelu(entries, approximate=True)


def slot_table(expert_ids, experts, capacity):
    flattened = expert_ids.reshape(-1)
    labels = jnp.arange(experts, dtype=jnp.int32)
    onehot = (flattened[:, None] == labels[None, :]).astype(jnp.int32)
    before = jnp.cumsum(onehot, axis=0) - onehot
    ranking = jnp.sum(before * onehot, axis=1)
    target = jnp.where(ranking < capacity, flattened * capacity + ranking, -1)
    places = jnp.arange(experts * capacity, dtype=jnp.int32)
    return (target[None, :] == places[:, None]).astype(BF16)


def place_rows(select, paired, experts, capacity):
    packed = jnp.dot(select, paired, preferred_element_type=F32).astype(BF16)
    return packed.reshape(experts, capacity, paired.shape[1])


def take_rows(select, landed):
    flattened = landed.reshape(-1, landed.shape[-1])
    return jnp.einsum("sp,sd->pd", select, flattened, preferred_element_type=F32)


def arrive(sent):
    landed = lax.all_to_all(sent, "exp", split_axis=0, concat_axis=0, tiled=True)
    return lax.all_gather(landed.reshape(-1, landed.shape[-1]), "rep", axis=0, tiled=True)


def depart(partial_value, experts, capacity):
    summed = lax.psum_scatter(partial_value.astype(BF16), "rep", scatter_dimension=0, tiled=True)
    return lax.all_to_all(
        summed.reshape(experts, capacity, summed.shape[-1]),
        "exp",
        split_axis=0,
        concat_axis=0,
        tiled=True,
    )


def local_general(tokens, gain, expert_ids, gates, w_in, w_out, cotangent):
    experts = lax.axis_size("exp")
    tok_count, features = tokens.shape
    capacity = max(2, 2 * tok_count // experts)
    values = tokens.astype(F32)
    normed, norm_back = jax.vjp(lambda entries: normalize(entries, gain), values)
    normed = normed.astype(BF16)
    select = slot_table(expert_ids, experts, capacity)
    x_sent = place_rows(select, jnp.repeat(normed, 2, axis=0), experts, capacity)
    scaled = (cotangent.astype(F32)[:, None, :] * gates[:, :, None]).astype(BF16)
    d_sent = place_rows(select, scaled.reshape(2 * tok_count, features), experts, capacity)
    w_first, w_second = w_in[0], w_out[0]
    in_rows = arrive(x_sent)
    preact = jnp.dot(in_rows, w_first, preferred_element_type=F32)
    activated, act_back = jax.vjp(activate, preact)
    hidden = activated.astype(BF16)
    y_back = depart(jnp.dot(hidden, w_second, preferred_element_type=F32), experts, capacity)
    grad_rows = arrive(d_sent)
    d_hidden = jnp.einsum("rd,fd->rf", grad_rows, w_second, preferred_element_type=F32)
    d_pre = act_back(d_hidden)[0].astype(BF16)
    grad_second = jnp.einsum("rf,rd->fd", hidden, grad_rows, preferred_element_type=F32)
    grad_first = jnp.einsum("rd,rf->df", in_rows, d_pre, preferred_element_type=F32)
    d_back = depart(
        jnp.einsum("rf,df->rd", d_pre, w_first, preferred_element_type=F32), experts, capacity
    )
    returned = take_rows(select, y_back).reshape(tok_count, 2, features)
    mixed = (values + jnp.sum(gates[:, :, None] * returned, axis=1)).astype(BF16)
    d_normed = jnp.sum(take_rows(select, d_back).reshape(tok_count, 2, features), axis=1)
    grad_tokens = (cotangent.astype(F32) + norm_back(d_normed)[0]).astype(BF16)
    return (mixed, grad_tokens, grad_first.astype(BF16)[None], grad_second.astype(BF16)[None])


def dot_nn(a, b):
    return jnp.dot(a, b, preferred_element_type=F32)


def dot_nt(a, b):
    return lax.dot_general(a, b, (((1,), (1,)), ((), ())), preferred_element_type=F32)


def dot_tn(a, b):
    return lax.dot_general(a, b, (((0,), (0,)), ((), ())), preferred_element_type=F32)


def slots_of(ids, me, experts, capacity):
    count = ids.shape[0]
    chips = experts // 2
    lanes = lax.broadcasted_iota(jnp.int32, (count, 128), 1)
    hit = [(ids[:, k : k + 1] == lanes).astype(F32) for k in range(2)]
    row = lax.broadcasted_iota(jnp.int32, (count, count), 0)
    col = lax.broadcasted_iota(jnp.int32, (count, count), 1)
    before = dot_nn((col < row).astype(BF16), (hit[0] + hit[1]).astype(BF16))
    slots = []
    for k in range(2):
        rank = jnp.sum(before * hit[k], axis=1, keepdims=True).astype(jnp.int32)
        label = ids[:, k : k + 1] ^ me
        block = (label & 1) * chips + (label >> 1)
        slots.append(jnp.where(rank < capacity, block * capacity + rank, -1))
    return slots


def row_stats(values):
    center = values - jnp.mean(values, axis=-1, keepdims=True)
    spread = jnp.mean(center * center, axis=-1, keepdims=True)
    return center, lax.rsqrt(spread + epsilon)


def send_kernel(experts, capacity, me_ref, tok_ref, gain_ref, ids_ref, gate_ref, cot_ref, keep_ref, swap_ref, slot_ref):
    count, features = tok_ref.shape
    half = experts // 2 * capacity
    slots = slots_of(ids_ref[...], me_ref[0], experts, capacity)
    lane = lax.broadcasted_iota(jnp.int32, (count, 2 * half), 1)
    picks = [(slots[k] == lane).astype(F32) for k in range(2)]
    slot_ref[...] = jnp.where(lax.broadcasted_iota(jnp.int32, (count, 2), 1) == 0, slots[0], slots[1])
    center, scale = row_stats(tok_ref[...].astype(F32))
    normed = (center * scale * gain_ref[...]).astype(BF16)
    cot = cot_ref[...].astype(F32)
    scaled = jnp.concatenate([(cot * gate_ref[:, k : k + 1]).astype(BF16) for k in range(2)], axis=0)
    pick_x = (picks[0] + picks[1]).astype(BF16)
    pick_d = jnp.concatenate([p.astype(BF16) for p in picks], axis=0)
    for part, out in ((1, swap_ref), (0, keep_ref)):
        at = slice(part * half, (part + 1) * half)
        out[:, :features] = dot_tn(pick_x[:, at], normed).astype(BF16)
        out[:, features:] = dot_tn(pick_d[:, at], scaled).astype(BF16)


def expert_kernel(o_ref, x_ref, y_ref, f_ref, w1_ref, w2_ref, p0_ref, s_ref, u_ref, hid_ref, pre_ref, *, order):
    count, width = o_ref.shape
    features = width // 2
    hidden_units = w1_ref.shape[1]
    tile = min(256, hidden_units)
    parts = (o_ref, x_ref, y_ref, f_ref)
    x_rows = jnp.concatenate([p[:, :features] for p in parts], axis=0)
    d_rows = jnp.concatenate([p[:, features:] for p in parts], axis=0)
    for j in range(0, hidden_units, tile):
        at = slice(j, j + tile)
        v = dot_nn(x_rows, w1_ref[:, at])
        dh = dot_nt(d_rows, w2_ref[at, :])
        v2 = v * v
        t = jnp.tanh(v * (ROOT_2_PI + (ROOT_2_PI * CUBIC) * v2))
        hid_ref[:, at] = (0.5 * v * (1.0 + t)).astype(BF16)
        slope = 0.5 * (1.0 + t) + 0.5 * v * (1.0 - t * t) * (ROOT_2_PI + (3.0 * ROOT_2_PI * CUBIC) * v2)
        pre_ref[:, at] = (dh * slope).astype(BF16)
    hid, pre = hid_ref[...], pre_ref[...]
    outs = (p0_ref, u_ref, s_ref, s_ref) if order == 0 else (p0_ref, s_ref, u_ref, s_ref)
    tops = (0, 0, 0, count)
    for j in range(0, features, tile):
        at = slice(j, j + tile)
        y = dot_nn(hid, w2_ref[:, at]).astype(BF16)
        dx = dot_nt(pre, w1_ref[at, :]).astype(BF16)
        for i in range(4):
            rows = slice(tops[i], tops[i] + count)
            outs[i][rows, at] = y[i * count : (i + 1) * count]
            outs[i][rows, features + j : features + j + tile] = dx[i * count : (i + 1) * count]


def grad_kernel(pieces, first, *refs):
    rows, tall, out_ref = refs[: 4 * pieces], refs[4 * pieces : 5 * pieces], refs[5 * pieces]
    step = pl.program_id(0)
    tile = out_ref.shape[0]
    features = rows[0].shape[1] // 2
    at = pl.ds(pl.multiple_of(step * tile, tile), tile)
    if first:
        left = jnp.concatenate([r[:, at] for r in rows], axis=0)
        right = jnp.concatenate([r[...] for r in tall], axis=0)
    else:
        left = jnp.concatenate([r[:, at] for r in tall], axis=0)
        right = jnp.concatenate([r[:, features:] for r in rows], axis=0)
    out_ref[...] = dot_tn(left, right).astype(BF16)


def last_kernel(capacity, slot_ref, tok_ref, gain_ref, gate_ref, cot_ref, *refs):
    pieces, other_ref, mixed_ref, grad_ref = refs[:-3], refs[-3], refs[-2], refs[-1]
    count, features = tok_ref.shape
    own = jnp.concatenate([p[:capacity] for p in pieces], axis=0)
    returned = jnp.concatenate([own, other_ref[...]], axis=0)
    lane = lax.broadcasted_iota(jnp.int32, (count, returned.shape[0]), 1)
    picks = [(slot_ref[:, k : k + 1] == lane).astype(F32) for k in range(2)]
    values = tok_ref[...].astype(F32)
    total = None
    for k in range(2):
        term = gate_ref[:, k : k + 1] * dot_nn(picks[k].astype(BF16), returned[:, :features])
        total = term if total is None else total + term
    mixed_ref[...] = (values + total).astype(BF16)
    d_normed = dot_nn((picks[0] + picks[1]).astype(BF16), returned[:, features:])
    center, scale = row_stats(values)
    down = d_normed * gain_ref[...]
    along = jnp.sum(down * center, axis=-1, keepdims=True) * (1.0 / features)
    d_center = down * scale - center * (scale * scale * scale * along)
    d_values = d_center - jnp.mean(d_center, axis=-1, keepdims=True)
    grad_ref[...] = (cot_ref[...].astype(F32) + d_values).astype(BF16)


def vmem(array):
    return pltpu.with_memory_space_constraint(array, pltpu.VMEM)


def call(kernel, outs, args, name, limit=24, **kwargs):
    spec = pl.BlockSpec(memory_space=pltpu.VMEM)
    return pl.pallas_call(
        kernel,
        out_shape=tuple(pltpu.VMEM(s, d) for s, d in outs),
        in_specs=[spec] * len(args),
        out_specs=tuple(spec for _ in outs),
        compiler_params=pltpu.CompilerParams(vmem_limit_bytes=limit << 20),
        name=name,
        **kwargs,
    )(*[vmem(a) for a in args])


def flip(array, axis_name, mask):
    size = lax.axis_size(axis_name)
    return lax.ppermute(array, axis_name, [(i, i ^ mask) for i in range(size)])


def f32(array):
    return array.astype(F32)


def local(tokens, gain, expert_ids, gates, w_in, w_out, cotangent):
    experts = lax.axis_size("exp")
    chips = experts // 2
    tok_count, features = tokens.shape
    capacity = max(2, 2 * tok_count // experts)
    me = lax.axis_index("exp").astype(jnp.int32).reshape(1)
    gain_row = gain.reshape(1, features)
    wide = 2 * features
    half = chips * capacity
    count = 2 * capacity
    spec = pl.BlockSpec(memory_space=pltpu.VMEM)
    keep, swap, slots = pl.pallas_call(
        functools.partial(send_kernel, experts, capacity),
        out_shape=(
            pltpu.VMEM((half, wide), BF16),
            pltpu.VMEM((half, wide), BF16),
            pltpu.VMEM((tok_count, 2), jnp.int32),
        ),
        in_specs=[pl.BlockSpec(memory_space=pltpu.SMEM)] + [spec] * 5,
        out_specs=(spec,) * 3,
        compiler_params=pltpu.CompilerParams(vmem_limit_bytes=24 << 20),
        name="send",
    )(me, tokens, gain_row, expert_ids, gates, cotangent)
    swapped = flip(swap, "exp", 1)
    w_first, w_second = w_in[0], w_out[0]
    chunk_order = (0, 1, 3, 2)
    landed = {}
    for k in chunk_order:
        at = slice(k * capacity, (k + 1) * capacity)
        own = jnp.concatenate([keep[at], swapped[at]], axis=0)
        landed[k] = flip(own, "exp", 2 * k) if k else own
    rows, tall, parts = {}, {}, {}
    for i, k in enumerate(chunk_order):
        order = i % 2
        own = landed[k]
        by_x, by_y = flip(own, "rep", 1), flip(own, "rep", 2)
        far = flip(by_y, "rep", 1) if order == 0 else flip(by_x, "rep", 2)
        rows[k] = (own, by_x, by_y, far)
        p0, s, u, hid, pre = call(
            functools.partial(expert_kernel, order=order),
            (
                ((count, wide), BF16),
                ((2 * count, wide), BF16),
                ((count, wide), BF16),
                ((4 * count, w_first.shape[1]), BF16),
                ((4 * count, w_first.shape[1]), BF16),
            ),
            (*rows[k], w_first, w_second),
            "expert",
        )
        tall[k] = (hid, pre)
        parts[k] = (p0, s, u, order)
    back = {}
    for k in (3, 2, 1, 0):
        p0, s, u, order = parts[k]
        near, then = (2, 1) if order == 0 else (1, 2)
        got = flip(s, "rep", near)
        got2 = flip((f32(u) + f32(got[count:])).astype(BF16), "rep", then)
        summed = (f32(p0) + f32(got[:count]) + f32(got2)).astype(BF16)
        back[k] = flip(summed, "exp", 2 * k) if k else summed
    grads = []
    for first in (False, True):
        args = [r for k in chunk_order for r in rows[k]] + [tall[k][1 if first else 0] for k in chunk_order]
        size = (features, w_first.shape[1]) if first else (w_first.shape[1], features)
        tile = min(256, size[0])
        grads.append(
            pl.pallas_call(
                functools.partial(grad_kernel, chips, first),
                out_shape=jax.ShapeDtypeStruct(size, BF16),
                grid=(size[0] // tile,),
                in_specs=[spec] * len(args),
                out_specs=pl.BlockSpec((tile, size[1]), lambda i: (i, 0)),
                compiler_params=pltpu.CompilerParams(vmem_limit_bytes=24 << 20),
                name="grad_in" if first else "grad_out",
                cost_estimate=pl.CostEstimate(
                    flops=2 * chips * 4 * count * size[0] * size[1],
                    bytes_accessed=2 * size[0] * size[1],
                    transcendentals=0,
                ),
            )(*[vmem(a) for a in args])
        )
    other = flip(jnp.concatenate([back[k][capacity:] for k in range(chips)], axis=0), "exp", 1)
    mixed, grad_tokens = pl.pallas_call(
        functools.partial(last_kernel, capacity),
        out_shape=(jax.ShapeDtypeStruct((tok_count, features), BF16),) * 2,
        in_specs=[spec] * (6 + chips),
        out_specs=(spec,) * 2,
        compiler_params=pltpu.CompilerParams(vmem_limit_bytes=24 << 20),
        name="last",
    )(vmem(slots), tokens, gain_row, gates, cotangent, *[vmem(back[k]) for k in range(chips)], vmem(other))
    return (mixed, grad_tokens, grads[1][None], grads[0][None])


def solution(mesh):
    rep, exp = mesh.shape["rep"], mesh.shape["exp"]

    def body(tokens, *rest):
        fits = rep == 4 and exp == 8 and (2 * tokens.shape[0] // exp) % 16 == 0
        return (local if fits else local_general)(tokens, *rest)

    return jax.shard_map(
        body,
        mesh=mesh,
        in_specs=(
            P(("rep", "exp"), None),
            P(),
            P(("rep", "exp"), None),
            P(("rep", "exp"), None),
            P("exp", None, "rep"),
            P("exp", "rep", None),
            P(("rep", "exp"), None),
        ),
        out_specs=(
            P(("rep", "exp"), None),
            P(("rep", "exp"), None),
            P("exp", None, "rep"),
            P("exp", "rep", None),
        ),
        check_vma=False,
    )
```

```python
import functools

import jax
import jax.numpy as jnp
from jax import lax
from jax.experimental import pallas as pl
from jax.experimental.pallas import tpu as pltpu
from jax.sharding import PartitionSpec as P


epsilon = 1e-05
ROOT_2_PI = 0.7978845608028654
CUBIC = 0.044715
BF16, F32 = jnp.bfloat16, jnp.float32
GATHER = (2, 2, 2, 2)
SCATTER = (2, 2, 2, 2)


def normalize(entries, gain):
    center = entries - jnp.mean(entries, axis=-1, keepdims=True)
    spread = jnp.mean(center * center, axis=-1, keepdims=True)
    return center * lax.rsqrt(spread + epsilon) * gain


def activate(entries):
    return jax.nn.gelu(entries, approximate=True)


def slot_table(expert_ids, experts, capacity):
    flattened = expert_ids.reshape(-1)
    labels = jnp.arange(experts, dtype=jnp.int32)
    onehot = (flattened[:, None] == labels[None, :]).astype(jnp.int32)
    before = jnp.cumsum(onehot, axis=0) - onehot
    ranking = jnp.sum(before * onehot, axis=1)
    target = jnp.where(ranking < capacity, flattened * capacity + ranking, -1)
    places = jnp.arange(experts * capacity, dtype=jnp.int32)
    return (target[None, :] == places[:, None]).astype(BF16)


def place_rows(select, paired, experts, capacity):
    packed = jnp.dot(select, paired, preferred_element_type=F32).astype(BF16)
    return packed.reshape(experts, capacity, paired.shape[1])


def take_rows(select, landed):
    flattened = landed.reshape(-1, landed.shape[-1])
    return jnp.einsum("sp,sd->pd", select, flattened, preferred_element_type=F32)


def arrive(sent):
    landed = lax.all_to_all(sent, "exp", split_axis=0, concat_axis=0, tiled=True)
    return lax.all_gather(landed.reshape(-1, landed.shape[-1]), "rep", axis=0, tiled=True)


def depart(partial_value, experts, capacity):
    summed = lax.psum_scatter(partial_value.astype(BF16), "rep", scatter_dimension=0, tiled=True)
    return lax.all_to_all(
        summed.reshape(experts, capacity, summed.shape[-1]),
        "exp",
        split_axis=0,
        concat_axis=0,
        tiled=True,
    )


def local_general(tokens, gain, expert_ids, gates, w_in, w_out, cotangent):
    experts = lax.axis_size("exp")
    tok_count, features = tokens.shape
    capacity = max(2, 2 * tok_count // experts)
    values = tokens.astype(F32)
    normed, norm_back = jax.vjp(lambda entries: normalize(entries, gain), values)
    normed = normed.astype(BF16)
    select = slot_table(expert_ids, experts, capacity)
    x_sent = place_rows(select, jnp.repeat(normed, 2, axis=0), experts, capacity)
    scaled = (cotangent.astype(F32)[:, None, :] * gates[:, :, None]).astype(BF16)
    d_sent = place_rows(select, scaled.reshape(2 * tok_count, features), experts, capacity)
    w_first, w_second = w_in[0], w_out[0]
    in_rows = arrive(x_sent)
    preact = jnp.dot(in_rows, w_first, preferred_element_type=F32)
    activated, act_back = jax.vjp(activate, preact)
    hidden = activated.astype(BF16)
    y_back = depart(jnp.dot(hidden, w_second, preferred_element_type=F32), experts, capacity)
    grad_rows = arrive(d_sent)
    d_hidden = jnp.einsum("rd,fd->rf", grad_rows, w_second, preferred_element_type=F32)
    d_pre = act_back(d_hidden)[0].astype(BF16)
    grad_second = jnp.einsum("rf,rd->fd", hidden, grad_rows, preferred_element_type=F32)
    grad_first = jnp.einsum("rd,rf->df", in_rows, d_pre, preferred_element_type=F32)
    d_back = depart(
        jnp.einsum("rf,df->rd", d_pre, w_first, preferred_element_type=F32), experts, capacity
    )
    returned = take_rows(select, y_back).reshape(tok_count, 2, features)
    mixed = (values + jnp.sum(gates[:, :, None] * returned, axis=1)).astype(BF16)
    d_normed = jnp.sum(take_rows(select, d_back).reshape(tok_count, 2, features), axis=1)
    grad_tokens = (cotangent.astype(F32) + norm_back(d_normed)[0]).astype(BF16)
    return (mixed, grad_tokens, grad_first.astype(BF16)[None], grad_second.astype(BF16)[None])


def dot_nn(a, b):
    return jnp.dot(a, b, preferred_element_type=F32)


def dot_nt(a, b):
    return lax.dot_general(a, b, (((1,), (1,)), ((), ())), preferred_element_type=F32)


def dot_tn(a, b):
    return lax.dot_general(a, b, (((0,), (0,)), ((), ())), preferred_element_type=F32)


def slots_of(ids, me, experts, capacity):
    count = ids[0].shape[0]
    chips = experts // 2
    lanes = lax.broadcasted_iota(jnp.int32, (count, 128), 1)
    hit = [(i == lanes).astype(F32) for i in ids]
    row = lax.broadcasted_iota(jnp.int32, (count, count), 0)
    col = lax.broadcasted_iota(jnp.int32, (count, count), 1)
    before = dot_nn((col < row).astype(BF16), (hit[0] + hit[1]).astype(BF16))
    slots = []
    for k in range(2):
        rank = jnp.sum(before * hit[k], axis=1, keepdims=True).astype(jnp.int32)
        label = ids[k] ^ me
        block = (label & 1) * chips + (label >> 1)
        slots.append(jnp.where(rank < capacity, block * capacity + rank, -1))
    return slots


def row_stats(values):
    center = values - jnp.mean(values, axis=-1, keepdims=True)
    spread = jnp.mean(center * center, axis=-1, keepdims=True)
    return center, lax.rsqrt(spread + epsilon)


def column(row):
    size = row.shape[1]
    here = lax.broadcasted_iota(jnp.int32, (size, size), 0) == lax.broadcasted_iota(jnp.int32, (size, size), 1)
    return jnp.sum(jnp.where(here, row, 0.0), axis=1, keepdims=True)


def send_kernel(experts, capacity, me_ref, *refs):
    sources, (keep_ref, swap_ref, slot_ref, gate_ref) = refs[:5], refs[5:9]
    landing, sems = refs[9:14], refs[14]
    copies = [pltpu.make_async_copy(a, b, sems.at[i]) for i, (a, b) in enumerate(zip(sources, landing))]
    for c in copies:
        c.start()
    id_rows, gate_rows, tok_ref, gain_ref, cot_ref = landing
    count, features = tok_ref.shape
    half = experts // 2 * capacity
    copies[0].wait()
    ids = [column(id_rows[k : k + 1, :].astype(F32)).astype(jnp.int32) for k in range(2)]
    slots = slots_of(ids, me_ref[0], experts, capacity)
    lane = lax.broadcasted_iota(jnp.int32, (count, 2 * half), 1)
    picks = [(slots[k] == lane).astype(F32) for k in range(2)]
    second = lax.broadcasted_iota(jnp.int32, (count, 2), 1) == 1
    slot_ref[...] = jnp.where(second, slots[1], slots[0])
    copies[1].wait()
    gates = [column(gate_rows[k : k + 1, :]) for k in range(2)]
    gate_ref[...] = jnp.where(second, gates[1], gates[0])
    copies[2].wait()
    copies[3].wait()
    center, scale = row_stats(tok_ref[...].astype(F32))
    normed = (center * scale * gain_ref[...]).astype(BF16)
    copies[4].wait()
    cot = cot_ref[...].astype(F32)
    scaled = jnp.concatenate([(cot * g).astype(BF16) for g in gates], axis=0)
    pick_x = (picks[0] + picks[1]).astype(BF16)
    pick_d = jnp.concatenate([p.astype(BF16) for p in picks], axis=0)
    for part, out in ((1, swap_ref), (0, keep_ref)):
        at = slice(part * half, (part + 1) * half)
        out[:, :features] = dot_tn(pick_x[:, at], normed).astype(BF16)
        out[:, features:] = dot_tn(pick_d[:, at], scaled).astype(BF16)


def expert_kernel(pieces, form, *refs):
    parts, (w1_ref, w2_ref), outs = refs[:pieces], refs[pieces : pieces + 2], refs[pieces + 2 : -2]
    hid_ref, pre_ref = refs[-2:]
    count, width = parts[0].shape
    features = width // 2
    hidden_units = w1_ref.shape[1]
    tile = min(256, hidden_units)
    x_rows = jnp.concatenate([p[:, :features] for p in parts], axis=0)
    d_rows = jnp.concatenate([p[:, features:] for p in parts], axis=0)
    for j in range(0, hidden_units, tile):
        at = slice(j, j + tile)
        v = dot_nn(x_rows, w1_ref[:, at])
        dh = dot_nt(d_rows, w2_ref[at, :])
        v2 = v * v
        t = jnp.tanh(v * (ROOT_2_PI + (ROOT_2_PI * CUBIC) * v2))
        hid_ref[:, at] = (0.5 * v * (1.0 + t)).astype(BF16)
        slope = 0.5 * (1.0 + t) + 0.5 * v * (1.0 - t * t) * (ROOT_2_PI + (3.0 * ROOT_2_PI * CUBIC) * v2)
        pre_ref[:, at] = (dh * slope).astype(BF16)
    hid, pre = hid_ref[...], pre_ref[...]
    half = count // 2
    if form == 2:
        moves = (
            (0, 0, count, 0, 0),
            (1, 0, half, 1, 0),
            (3, 0, half, 1, half),
            (2, half, count, 2, 0),
            (3, half, count, 2, half),
            (2, 0, half, 3, 0),
            (1, half, count, 4, 0),
        )
    else:
        near, then = (2, 1) if form == 0 else (1, 2)
        moves = ((0, 0, count, 0, 0), (near, 0, count, 1, 0), (3, 0, count, 1, count), (then, 0, count, 2, 0))
    for j in range(0, features, tile):
        y = dot_nn(hid, w2_ref[:, j : j + tile]).astype(BF16)
        dx = dot_nt(pre, w1_ref[j : j + tile, :]).astype(BF16)
        for rep, low, high, out, to in moves:
            rows, there = slice(rep * count + low, rep * count + high), slice(to, to + high - low)
            outs[out][there, j : j + tile] = y[rows]
            outs[out][there, features + j : features + j + tile] = dx[rows]


def grad_kernel(pieces, chips, first, *refs):
    rows, tall, out_ref = refs[:pieces], refs[pieces : pieces + chips], refs[pieces + chips]
    step = pl.program_id(0)
    tile = out_ref.shape[0]
    features = rows[0].shape[1] // 2
    at = pl.ds(pl.multiple_of(step * tile, tile), tile)
    if first:
        left = jnp.concatenate([r[:, at] for r in rows], axis=0)
        right = jnp.concatenate([r[...] for r in tall], axis=0)
    else:
        left = jnp.concatenate([r[:, at] for r in tall], axis=0)
        right = jnp.concatenate([r[:, features:] for r in rows], axis=0)
    out_ref[...] = dot_tn(left, right).astype(BF16)


def last_kernel(capacity, slot_ref, tok_ref, gain_ref, gate_ref, cot_ref, *refs):
    pieces, other_ref, mixed_ref, grad_ref = refs[:-3], refs[-3], refs[-2], refs[-1]
    count, features = tok_ref.shape
    own = jnp.concatenate([p[:capacity] for p in pieces], axis=0)
    returned = jnp.concatenate([own, other_ref[...]], axis=0)
    lane = lax.broadcasted_iota(jnp.int32, (count, returned.shape[0]), 1)
    picks = [(slot_ref[:, k : k + 1] == lane).astype(F32) for k in range(2)]
    values = tok_ref[...].astype(F32)
    total = None
    for k in range(2):
        term = gate_ref[:, k : k + 1] * dot_nn(picks[k].astype(BF16), returned[:, :features])
        total = term if total is None else total + term
    mixed_ref[...] = (values + total).astype(BF16)
    d_normed = dot_nn((picks[0] + picks[1]).astype(BF16), returned[:, features:])
    center, scale = row_stats(values)
    down = d_normed * gain_ref[...]
    along = jnp.sum(down * center, axis=-1, keepdims=True) * (1.0 / features)
    d_center = down * scale - center * (scale * scale * scale * along)
    d_values = d_center - jnp.mean(d_center, axis=-1, keepdims=True)
    grad_ref[...] = (cot_ref[...].astype(F32) + d_values).astype(BF16)


def vmem(array):
    return pltpu.with_memory_space_constraint(array, pltpu.VMEM)


def call(kernel, outs, args, limit=24, **kwargs):
    spec = pl.BlockSpec(memory_space=pltpu.VMEM)
    return pl.pallas_call(
        kernel,
        out_shape=tuple(pltpu.VMEM(s, d) for s, d in outs),
        in_specs=[spec] * len(args),
        out_specs=tuple(spec for _ in outs),
        compiler_params=pltpu.CompilerParams(vmem_limit_bytes=limit << 20),
        **kwargs,
    )(*[vmem(a) for a in args])


def flip(array, axis_name, mask):
    size = lax.axis_size(axis_name)
    return lax.ppermute(array, axis_name, [(i, i ^ mask) for i in range(size)])


def f32(array):
    return array.astype(F32)


def local(tokens, gain, expert_ids, gates, w_in, w_out, cotangent):
    return local_inner(tokens, gain, expert_ids, gates, w_in, w_out, cotangent)


def local_inner(tokens, gain, expert_ids, gates, w_in, w_out, cotangent):
    experts = lax.axis_size("exp")
    chips = experts // 2
    tok_count, features = tokens.shape
    capacity = max(2, 2 * tok_count // experts)
    me = lax.axis_index("exp").astype(jnp.int32).reshape(1)
    gain_row = gain.reshape(1, features)
    wide = 2 * features
    half = chips * capacity
    count = 2 * capacity
    spec = pl.BlockSpec(memory_space=pltpu.VMEM)
    there = [pltpu.with_memory_space_constraint(a, pltpu.HBM) for a in (expert_ids.T, gates.T, tokens, gain_row, cotangent)]
    keep, swap, slots, gate_columns = pl.pallas_call(
        functools.partial(send_kernel, experts, capacity),
        out_shape=(
            pltpu.VMEM((half, wide), BF16),
            pltpu.VMEM((half, wide), BF16),
            pltpu.VMEM((tok_count, 2), jnp.int32),
            pltpu.VMEM((tok_count, 2), F32),
        ),
        in_specs=[pl.BlockSpec(memory_space=pltpu.SMEM)] + [pl.BlockSpec(memory_space=pltpu.HBM)] * 5,
        out_specs=(spec,) * 4,
        scratch_shapes=[pltpu.VMEM(a.shape, a.dtype) for a in there] + [pltpu.SemaphoreType.DMA((5,))],
        compiler_params=pltpu.CompilerParams(vmem_limit_bytes=16 << 20),
        name="send",
    )(me, *there)
    swapped = flip(swap, "exp", 1)
    w_first, w_second = w_in[0], w_out[0]
    units = w_first.shape[1]
    landed = {}
    for k in range(chips):
        at = slice(k * capacity, (k + 1) * capacity)
        own = jnp.concatenate([keep[at], swapped[at]], axis=0)
        landed[k] = flip(own, "exp", 2 * k) if k else own
    rows, tall, parts = {}, {}, {}
    for k in range(chips):
        own = landed[k]
        by_x, by_y = flip(own, "rep", 1), flip(own, "rep", 2)
        if GATHER[k] == 0:
            far = (flip(by_y, "rep", 1),)
        elif GATHER[k] == 1:
            far = (flip(by_x, "rep", 2),)
        else:
            far = (flip(by_y[:capacity], "rep", 1), flip(by_x[capacity:], "rep", 2))
        rows[k] = (own, by_x, by_y, *far)
        sizes = (count, count, count, capacity, capacity) if SCATTER[k] == 2 else (count, 2 * count, count)
        *leaving, hid, pre = call(
            functools.partial(expert_kernel, len(rows[k]), SCATTER[k]),
            tuple(((n, wide), BF16) for n in sizes) + (((4 * count, units), BF16),) * 2,
            (*rows[k], w_first, w_second),
            cost_estimate=pl.CostEstimate(
                flops=8 * 4 * count * features * units, bytes_accessed=4 * features * units, transcendentals=0
            ),
        )
        tall[k], parts[k] = (hid, pre), leaving
    back = {}
    for k in range(chips):
        if SCATTER[k] == 2:
            own, to_x, to_y, via_y, via_x = parts[k]
            got_x, got_y = flip(to_x, "rep", 1), flip(to_y, "rep", 2)
            last_a = flip((f32(via_y) + f32(got_x[capacity:])).astype(BF16), "rep", 2)
            last_b = flip((f32(via_x) + f32(got_y[capacity:])).astype(BF16), "rep", 1)
            near = jnp.concatenate([got_x[:capacity], got_y[:capacity]], axis=0)
            summed = (f32(own) + f32(near) + f32(jnp.concatenate([last_a, last_b], axis=0))).astype(BF16)
        else:
            own, near, then = parts[k]
            first, second = (2, 1) if SCATTER[k] == 0 else (1, 2)
            got = flip(near, "rep", first)
            last = flip((f32(then) + f32(got[count:])).astype(BF16), "rep", second)
            summed = (f32(own) + f32(got[:count]) + f32(last)).astype(BF16)
        back[k] = flip(summed, "exp", 2 * k) if k else summed
    grads = []
    pieces = [r for k in range(chips) for r in rows[k]]
    for first in (False, True):
        args = pieces + [tall[k][1 if first else 0] for k in range(chips)]
        size = (features, units) if first else (units, features)
        tile = min(256, size[0])
        grads.append(
            pl.pallas_call(
                functools.partial(grad_kernel, len(pieces), chips, first),
                out_shape=jax.ShapeDtypeStruct(size, BF16),
                grid=(size[0] // tile,),
                in_specs=[spec] * len(args),
                out_specs=pl.BlockSpec((tile, size[1]), lambda i: (i, 0)),
                compiler_params=pltpu.CompilerParams(vmem_limit_bytes=24 << 20),
                name="grad_in" if first else "grad_out",
                cost_estimate=pl.CostEstimate(
                    flops=2 * chips * 4 * count * size[0] * size[1],
                    bytes_accessed=2 * size[0] * size[1],
                    transcendentals=0,
                ),
            )(*[vmem(a) for a in args])
        )
    other = flip(jnp.concatenate([back[k][capacity:] for k in range(chips)], axis=0), "exp", 1)
    mixed, grad_tokens = pl.pallas_call(
        functools.partial(last_kernel, capacity),
        out_shape=(jax.ShapeDtypeStruct((tok_count, features), BF16),) * 2,
        in_specs=[spec] * (6 + chips),
        out_specs=(spec,) * 2,
        compiler_params=pltpu.CompilerParams(vmem_limit_bytes=24 << 20),
        name="last",
    )(vmem(slots), tokens, gain_row, vmem(gate_columns), cotangent, *[vmem(back[k]) for k in range(chips)], vmem(other))
    return (mixed, grad_tokens, grads[1][None], grads[0][None])


def solution(mesh):
    rep, exp = mesh.shape["rep"], mesh.shape["exp"]

    def body(tokens, *rest):
        fits = rep == 4 and exp == 8 and (2 * tokens.shape[0] // exp) % 16 == 0
        return (local if fits else local_general)(tokens, *rest)

    return jax.shard_map(
        body,
        mesh=mesh,
        in_specs=(
            P(("rep", "exp"), None),
            P(),
            P(("rep", "exp"), None),
            P(("rep", "exp"), None),
            P("exp", None, "rep"),
            P("exp", "rep", None),
            P(("rep", "exp"), None),
        ),
        out_specs=(
            P(("rep", "exp"), None),
            P(("rep", "exp"), None),
            P("exp", None, "rep"),
            P("exp", "rep", None),
        ),
        check_vma=False,
    )
```

```python
import functools

import jax
import jax.numpy as jnp
from jax import lax
from jax.experimental import pallas as pl
from jax.experimental.pallas import tpu as pltpu
from jax.sharding import PartitionSpec as P


epsilon = 1e-05
ROOT_2_PI = 0.7978845608028654
CUBIC = 0.044715
BF16, F32 = jnp.bfloat16, jnp.float32
GATHER = (2, 2, 2, 2)
SCATTER = (3, 2, 3, 2)


def normalize(entries, gain):
    center = entries - jnp.mean(entries, axis=-1, keepdims=True)
    spread = jnp.mean(center * center, axis=-1, keepdims=True)
    return center * lax.rsqrt(spread + epsilon) * gain


def activate(entries):
    return jax.nn.gelu(entries, approximate=True)


def slot_table(expert_ids, experts, capacity):
    flattened = expert_ids.reshape(-1)
    labels = jnp.arange(experts, dtype=jnp.int32)
    onehot = (flattened[:, None] == labels[None, :]).astype(jnp.int32)
    before = jnp.cumsum(onehot, axis=0) - onehot
    ranking = jnp.sum(before * onehot, axis=1)
    target = jnp.where(ranking < capacity, flattened * capacity + ranking, -1)
    places = jnp.arange(experts * capacity, dtype=jnp.int32)
    return (target[None, :] == places[:, None]).astype(BF16)


def place_rows(select, paired, experts, capacity):
    packed = jnp.dot(select, paired, preferred_element_type=F32).astype(BF16)
    return packed.reshape(experts, capacity, paired.shape[1])


def take_rows(select, landed):
    flattened = landed.reshape(-1, landed.shape[-1])
    return jnp.einsum("sp,sd->pd", select, flattened, preferred_element_type=F32)


def arrive(sent):
    landed = lax.all_to_all(sent, "exp", split_axis=0, concat_axis=0, tiled=True)
    return lax.all_gather(landed.reshape(-1, landed.shape[-1]), "rep", axis=0, tiled=True)


def depart(partial_value, experts, capacity):
    summed = lax.psum_scatter(partial_value.astype(BF16), "rep", scatter_dimension=0, tiled=True)
    return lax.all_to_all(
        summed.reshape(experts, capacity, summed.shape[-1]),
        "exp",
        split_axis=0,
        concat_axis=0,
        tiled=True,
    )


def local_general(tokens, gain, expert_ids, gates, w_in, w_out, cotangent):
    experts = lax.axis_size("exp")
    tok_count, features = tokens.shape
    capacity = max(2, 2 * tok_count // experts)
    values = tokens.astype(F32)
    normed, norm_back = jax.vjp(lambda entries: normalize(entries, gain), values)
    normed = normed.astype(BF16)
    select = slot_table(expert_ids, experts, capacity)
    x_sent = place_rows(select, jnp.repeat(normed, 2, axis=0), experts, capacity)
    scaled = (cotangent.astype(F32)[:, None, :] * gates[:, :, None]).astype(BF16)
    d_sent = place_rows(select, scaled.reshape(2 * tok_count, features), experts, capacity)
    w_first, w_second = w_in[0], w_out[0]
    in_rows = arrive(x_sent)
    preact = jnp.dot(in_rows, w_first, preferred_element_type=F32)
    activated, act_back = jax.vjp(activate, preact)
    hidden = activated.astype(BF16)
    y_back = depart(jnp.dot(hidden, w_second, preferred_element_type=F32), experts, capacity)
    grad_rows = arrive(d_sent)
    d_hidden = jnp.einsum("rd,fd->rf", grad_rows, w_second, preferred_element_type=F32)
    d_pre = act_back(d_hidden)[0].astype(BF16)
    grad_second = jnp.einsum("rf,rd->fd", hidden, grad_rows, preferred_element_type=F32)
    grad_first = jnp.einsum("rd,rf->df", in_rows, d_pre, preferred_element_type=F32)
    d_back = depart(
        jnp.einsum("rf,df->rd", d_pre, w_first, preferred_element_type=F32), experts, capacity
    )
    returned = take_rows(select, y_back).reshape(tok_count, 2, features)
    mixed = (values + jnp.sum(gates[:, :, None] * returned, axis=1)).astype(BF16)
    d_normed = jnp.sum(take_rows(select, d_back).reshape(tok_count, 2, features), axis=1)
    grad_tokens = (cotangent.astype(F32) + norm_back(d_normed)[0]).astype(BF16)
    return (mixed, grad_tokens, grad_first.astype(BF16)[None], grad_second.astype(BF16)[None])


def dot_nn(a, b):
    return jnp.dot(a, b, preferred_element_type=F32)


def dot_nt(a, b):
    return lax.dot_general(a, b, (((1,), (1,)), ((), ())), preferred_element_type=F32)


def dot_tn(a, b):
    return lax.dot_general(a, b, (((0,), (0,)), ((), ())), preferred_element_type=F32)


def slots_of(ids, me, experts, capacity):
    count = ids[0].shape[0]
    chips = experts // 2
    lanes = lax.broadcasted_iota(jnp.int32, (count, 128), 1)
    hit = [(i == lanes).astype(F32) for i in ids]
    row = lax.broadcasted_iota(jnp.int32, (count, count), 0)
    col = lax.broadcasted_iota(jnp.int32, (count, count), 1)
    before = dot_nn((col < row).astype(BF16), (hit[0] + hit[1]).astype(BF16))
    slots = []
    for k in range(2):
        rank = jnp.sum(before * hit[k], axis=1, keepdims=True).astype(jnp.int32)
        label = ids[k] ^ me
        block = (label & 1) * chips + (label >> 1)
        slots.append(jnp.where(rank < capacity, block * capacity + rank, -1))
    return slots


def row_stats(values):
    center = values - jnp.mean(values, axis=-1, keepdims=True)
    spread = jnp.mean(center * center, axis=-1, keepdims=True)
    return center, lax.rsqrt(spread + epsilon)


def column(row):
    size = row.shape[1]
    here = lax.broadcasted_iota(jnp.int32, (size, size), 0) == lax.broadcasted_iota(jnp.int32, (size, size), 1)
    return jnp.sum(jnp.where(here, row, 0.0), axis=1, keepdims=True)


def send_kernel(experts, capacity, me_ref, *refs):
    sources, (keep_ref, swap_ref, slot_ref, gate_ref) = refs[:5], refs[5:9]
    landing, sems = refs[9:14], refs[14]
    copies = [pltpu.make_async_copy(a, b, sems.at[i]) for i, (a, b) in enumerate(zip(sources, landing))]
    for c in copies:
        c.start()
    id_rows, gate_rows, tok_ref, gain_ref, cot_ref = landing
    count, features = tok_ref.shape
    half = experts // 2 * capacity
    copies[0].wait()
    ids = [column(id_rows[k : k + 1, :].astype(F32)).astype(jnp.int32) for k in range(2)]
    slots = slots_of(ids, me_ref[0], experts, capacity)
    lane = lax.broadcasted_iota(jnp.int32, (count, 2 * half), 1)
    picks = [(slots[k] == lane).astype(F32) for k in range(2)]
    second = lax.broadcasted_iota(jnp.int32, (count, 2), 1) == 1
    slot_ref[...] = jnp.where(second, slots[1], slots[0])
    copies[1].wait()
    gates = [column(gate_rows[k : k + 1, :]) for k in range(2)]
    gate_ref[...] = jnp.where(second, gates[1], gates[0])
    copies[2].wait()
    copies[3].wait()
    center, scale = row_stats(tok_ref[...].astype(F32))
    normed = (center * scale * gain_ref[...]).astype(BF16)
    copies[4].wait()
    cot = cot_ref[...].astype(F32)
    scaled = jnp.concatenate([(cot * g).astype(BF16) for g in gates], axis=0)
    pick_x = (picks[0] + picks[1]).astype(BF16)
    pick_d = jnp.concatenate([p.astype(BF16) for p in picks], axis=0)
    for part, out in ((1, swap_ref), (0, keep_ref)):
        at = slice(part * half, (part + 1) * half)
        out[:, :features] = dot_tn(pick_x[:, at], normed).astype(BF16)
        out[:, features:] = dot_tn(pick_d[:, at], scaled).astype(BF16)


def expert_kernel(pieces, form, *refs):
    parts, (w1_ref, w2_ref), outs = refs[:pieces], refs[pieces : pieces + 2], refs[pieces + 2 : -2]
    hid_ref, pre_ref = refs[-2:]
    count, width = parts[0].shape
    features = width // 2
    hidden_units = w1_ref.shape[1]
    tile = min(256, hidden_units)
    x_rows = jnp.concatenate([p[:, :features] for p in parts], axis=0)
    d_rows = jnp.concatenate([p[:, features:] for p in parts], axis=0)
    for j in range(0, hidden_units, tile):
        at = slice(j, j + tile)
        v = dot_nn(x_rows, w1_ref[:, at])
        dh = dot_nt(d_rows, w2_ref[at, :])
        v2 = v * v
        t = jnp.tanh(v * (ROOT_2_PI + (ROOT_2_PI * CUBIC) * v2))
        hid_ref[:, at] = (0.5 * v * (1.0 + t)).astype(BF16)
        slope = 0.5 * (1.0 + t) + 0.5 * v * (1.0 - t * t) * (ROOT_2_PI + (3.0 * ROOT_2_PI * CUBIC) * v2)
        pre_ref[:, at] = (dh * slope).astype(BF16)
    hid, pre = hid_ref[...], pre_ref[...]
    half = count // 2
    if form == 3:
        moves = (
            (0, 0, half, 0, 0),
            (1, 0, half, 1, 0),
            (3, 0, half, 1, half),
            (2, 0, half, 2, 0),
            (2, half, count, 3, 0),
            (3, half, count, 3, half),
            (1, half, count, 3, count),
            (0, half, count, 3, count + half),
        )
    elif form == 2:
        moves = (
            (0, 0, count, 0, 0),
            (1, 0, half, 1, 0),
            (3, 0, half, 1, half),
            (2, half, count, 2, 0),
            (3, half, count, 2, half),
            (2, 0, half, 3, 0),
            (1, half, count, 4, 0),
        )
    else:
        near, then = (2, 1) if form == 0 else (1, 2)
        moves = ((0, 0, count, 0, 0), (near, 0, count, 1, 0), (3, 0, count, 1, count), (then, 0, count, 2, 0))
    for j in range(0, features, tile):
        y = dot_nn(hid, w2_ref[:, j : j + tile]).astype(BF16)
        dx = dot_nt(pre, w1_ref[j : j + tile, :]).astype(BF16)
        for rep, low, high, out, to in moves:
            rows, there = slice(rep * count + low, rep * count + high), slice(to, to + high - low)
            outs[out][there, j : j + tile] = y[rows]
            outs[out][there, features + j : features + j + tile] = dx[rows]


def grad_kernel(pieces, chips, first, base, *refs):
    if base:
        refs = refs[1:]
    rows, tall, out_ref = refs[:pieces], refs[pieces : pieces + chips], refs[pieces + chips]
    step = pl.program_id(0) + base
    tile = out_ref.shape[0]
    features = rows[0].shape[1] // 2
    at = pl.ds(pl.multiple_of(step * tile, tile), tile)
    if first:
        left = jnp.concatenate([r[:, at] for r in rows], axis=0)
        right = jnp.concatenate([r[...] for r in tall], axis=0)
    else:
        left = jnp.concatenate([r[:, at] for r in tall], axis=0)
        right = jnp.concatenate([r[:, features:] for r in rows], axis=0)
    out_ref[...] = dot_tn(left, right).astype(BF16)


def last_kernel(capacity, chips, late, slot_ref, tok_ref, gain_ref, gate_ref, cot_ref, *refs):
    pieces, mixed_ref, grad_ref = refs[:-2], refs[-2], refs[-1]
    count, features = tok_ref.shape
    odd = [pieces[k][capacity:] for k in range(chips)]
    for i, k in enumerate(late):
        odd[k] = pieces[chips][i * capacity : (i + 1) * capacity]
    returned = jnp.concatenate([p[:capacity] for p in pieces[:chips]] + odd, axis=0)
    lane = lax.broadcasted_iota(jnp.int32, (count, returned.shape[0]), 1)
    picks = [(slot_ref[:, k : k + 1] == lane).astype(F32) for k in range(2)]
    values = tok_ref[...].astype(F32)
    total = None
    for k in range(2):
        term = gate_ref[:, k : k + 1] * dot_nn(picks[k].astype(BF16), returned[:, :features])
        total = term if total is None else total + term
    mixed_ref[...] = (values + total).astype(BF16)
    d_normed = dot_nn((picks[0] + picks[1]).astype(BF16), returned[:, features:])
    center, scale = row_stats(values)
    down = d_normed * gain_ref[...]
    along = jnp.sum(down * center, axis=-1, keepdims=True) * (1.0 / features)
    d_center = down * scale - center * (scale * scale * scale * along)
    d_values = d_center - jnp.mean(d_center, axis=-1, keepdims=True)
    grad_ref[...] = (cot_ref[...].astype(F32) + d_values).astype(BF16)


def vmem(array):
    return pltpu.with_memory_space_constraint(array, pltpu.VMEM)


def call(kernel, outs, args, limit=24, **kwargs):
    spec = pl.BlockSpec(memory_space=pltpu.VMEM)
    return pl.pallas_call(
        kernel,
        out_shape=tuple(pltpu.VMEM(s, d) for s, d in outs),
        in_specs=[spec] * len(args),
        out_specs=tuple(spec for _ in outs),
        compiler_params=pltpu.CompilerParams(vmem_limit_bytes=limit << 20),
        **kwargs,
    )(*[vmem(a) for a in args])


def flip(array, axis_name, mask):
    size = lax.axis_size(axis_name)
    return lax.ppermute(array, axis_name, [(i, i ^ mask) for i in range(size)])


def f32(array):
    return array.astype(F32)


def local(tokens, gain, expert_ids, gates, w_in, w_out, cotangent):
    return local_inner(tokens, gain, expert_ids, gates, w_in, w_out, cotangent)


def local_inner(tokens, gain, expert_ids, gates, w_in, w_out, cotangent):
    experts = lax.axis_size("exp")
    chips = experts // 2
    tok_count, features = tokens.shape
    capacity = max(2, 2 * tok_count // experts)
    me = lax.axis_index("exp").astype(jnp.int32).reshape(1)
    gain_row = gain.reshape(1, features)
    wide = 2 * features
    half = chips * capacity
    count = 2 * capacity
    spec = pl.BlockSpec(memory_space=pltpu.VMEM)
    there = [pltpu.with_memory_space_constraint(a, pltpu.HBM) for a in (expert_ids.T, gates.T, tokens, gain_row, cotangent)]
    keep, swap, slots, gate_columns = pl.pallas_call(
        functools.partial(send_kernel, experts, capacity),
        out_shape=(
            pltpu.VMEM((half, wide), BF16),
            pltpu.VMEM((half, wide), BF16),
            pltpu.VMEM((tok_count, 2), jnp.int32),
            pltpu.VMEM((tok_count, 2), F32),
        ),
        in_specs=[pl.BlockSpec(memory_space=pltpu.SMEM)] + [pl.BlockSpec(memory_space=pltpu.HBM)] * 5,
        out_specs=(spec,) * 4,
        scratch_shapes=[pltpu.VMEM(a.shape, a.dtype) for a in there] + [pltpu.SemaphoreType.DMA((5,))],
        compiler_params=pltpu.CompilerParams(vmem_limit_bytes=16 << 20),
        name="send",
    )(me, *there)
    swapped = flip(swap, "exp", 1)
    w_first, w_second = w_in[0], w_out[0]
    units = w_first.shape[1]
    landed = {}
    for k in range(chips):
        at = slice(k * capacity, (k + 1) * capacity)
        own = jnp.concatenate([keep[at], swapped[at]], axis=0)
        landed[k] = flip(own, "exp", 2 * k) if k else own
    rows, tall, parts = {}, {}, {}
    for k in range(chips):
        own = landed[k]
        by_x, by_y = flip(own, "rep", 1), flip(own, "rep", 2)
        if GATHER[k] == 0:
            far = (flip(by_y, "rep", 1),)
        elif GATHER[k] == 1:
            far = (flip(by_x, "rep", 2),)
        else:
            far = (flip(by_y[:capacity], "rep", 1), flip(by_x[capacity:], "rep", 2))
        rows[k] = (own, by_x, by_y, *far)
        if SCATTER[k] == 3:
            sizes = (capacity, count, capacity, 2 * count)
        else:
            sizes = (count, count, count, capacity, capacity) if SCATTER[k] == 2 else (count, 2 * count, count)
        *leaving, hid, pre = call(
            functools.partial(expert_kernel, len(rows[k]), SCATTER[k]),
            tuple(((n, wide), BF16) for n in sizes) + (((4 * count, units), BF16),) * 2,
            (*rows[k], w_first, w_second),
            cost_estimate=pl.CostEstimate(
                flops=8 * 4 * count * features * units, bytes_accessed=4 * features * units, transcendentals=0
            ),
        )
        tall[k], parts[k] = (hid, pre), leaving
    back = {}
    for k in range(chips):
        if SCATTER[k] >= 2:
            if SCATTER[k] == 3:
                own, to_x, via_y, swap_k = parts[k]
                swap_k = flip(swap_k, "exp", 1)
                to_y = swap_k[:count]
                via_x = swap_k[count : count + capacity]
                own = jnp.concatenate([own, swap_k[count + capacity :]], axis=0)
            else:
                own, to_x, to_y, via_y, via_x = parts[k]
            got_x, got_y = flip(to_x, "rep", 1), flip(to_y, "rep", 2)
            sum_a = (f32(via_y) + f32(got_x[capacity:])).astype(BF16)
            sum_b = (f32(via_x) + f32(got_y[capacity:])).astype(BF16)
            last_a, last_b = flip(sum_a, "rep", 2), flip(sum_b, "rep", 1)
            near = jnp.concatenate([got_x[:capacity], got_y[:capacity]], axis=0)
            summed = (f32(own) + f32(near) + f32(jnp.concatenate([last_a, last_b], axis=0))).astype(BF16)
        else:
            own, near, then = parts[k]
            first, second = (2, 1) if SCATTER[k] == 0 else (1, 2)
            got = flip(near, "rep", first)
            last = flip((f32(then) + f32(got[count:])).astype(BF16), "rep", second)
            summed = (f32(own) + f32(got[:count]) + f32(last)).astype(BF16)
        back[k] = flip(summed, "exp", 2 * k) if k else summed
    grads = []
    pieces = [r for k in range(chips) for r in rows[k]]
    for first in (False, True):
        args = [vmem(a) for a in pieces + [tall[k][1 if first else 0] for k in range(chips)]]
        size = (features, units) if first else (units, features)
        tile = min(256, size[0])
        steps = size[0] // tile
        done = None
        for base in (0, steps // 2):
            done = pl.pallas_call(
                functools.partial(grad_kernel, len(pieces), chips, first, base),
                out_shape=jax.ShapeDtypeStruct(size, BF16),
                grid=(steps - base if base else steps // 2,),
                in_specs=([pl.BlockSpec(memory_space=pl.ANY)] if base else []) + [spec] * len(args),
                out_specs=pl.BlockSpec((tile, size[1]), lambda i, base=base: (i + base, 0)),
                input_output_aliases={0: 0} if base else {},
                compiler_params=pltpu.CompilerParams(vmem_limit_bytes=24 << 20),
                name="grad_in" if first else "grad_out",
                cost_estimate=pl.CostEstimate(
                    flops=chips * 4 * count * size[0] * size[1],
                    bytes_accessed=size[0] * size[1],
                    transcendentals=0,
                ),
            )(*([done] if base else []), *args)
        grads.append(done)
    late = [k for k in range(chips) if SCATTER[k] != 3]
    other = flip(jnp.concatenate([back[k][capacity:] for k in late], axis=0), "exp", 1) if late else None
    ready = [vmem(back[k]) for k in range(chips)]
    if late:
        ready.append(vmem(other))
    mixed, grad_tokens = pl.pallas_call(
        functools.partial(last_kernel, capacity, chips, late),
        out_shape=(jax.ShapeDtypeStruct((tok_count, features), BF16),) * 2,
        in_specs=[spec] * (5 + len(ready)),
        out_specs=(spec,) * 2,
        compiler_params=pltpu.CompilerParams(vmem_limit_bytes=24 << 20),
        name="last",
    )(
        vmem(slots),
        tokens,
        gain_row,
        vmem(gate_columns),
        cotangent,
        *ready,
    )
    return (mixed, grad_tokens, grads[1][None], grads[0][None])


def solution(mesh):
    rep, exp = mesh.shape["rep"], mesh.shape["exp"]

    def body(tokens, *rest):
        fits = rep == 4 and exp == 8 and (2 * tokens.shape[0] // exp) % 16 == 0
        return (local if fits else local_general)(tokens, *rest)

    return jax.shard_map(
        body,
        mesh=mesh,
        in_specs=(
            P(("rep", "exp"), None),
            P(),
            P(("rep", "exp"), None),
            P(("rep", "exp"), None),
            P("exp", None, "rep"),
            P("exp", "rep", None),
            P(("rep", "exp"), None),
        ),
        out_specs=(
            P(("rep", "exp"), None),
            P(("rep", "exp"), None),
            P("exp", None, "rep"),
            P("exp", "rep", None),
        ),
        check_vma=False,
    )
```

```python
import functools

import jax
import jax.numpy as jnp
from jax import lax
from jax.experimental import pallas as pl
from jax.experimental.pallas import tpu as pltpu
from jax.sharding import PartitionSpec as P


epsilon = 1e-05
ROOT_2_PI = 0.7978845608028654
CUBIC = 0.044715
BF16, F32 = jnp.bfloat16, jnp.float32
GATHER = (2, 2, 2, 2)
SCATTER = (3, 2, 3, 2)


def normalize(entries, gain):
    center = entries - jnp.mean(entries, axis=-1, keepdims=True)
    spread = jnp.mean(center * center, axis=-1, keepdims=True)
    return center * lax.rsqrt(spread + epsilon) * gain


def activate(entries):
    return jax.nn.gelu(entries, approximate=True)


def slot_table(expert_ids, experts, capacity):
    flattened = expert_ids.reshape(-1)
    labels = jnp.arange(experts, dtype=jnp.int32)
    onehot = (flattened[:, None] == labels[None, :]).astype(jnp.int32)
    before = jnp.cumsum(onehot, axis=0) - onehot
    ranking = jnp.sum(before * onehot, axis=1)
    target = jnp.where(ranking < capacity, flattened * capacity + ranking, -1)
    places = jnp.arange(experts * capacity, dtype=jnp.int32)
    return (target[None, :] == places[:, None]).astype(BF16)


def place_rows(select, paired, experts, capacity):
    packed = jnp.dot(select, paired, preferred_element_type=F32).astype(BF16)
    return packed.reshape(experts, capacity, paired.shape[1])


def take_rows(select, landed):
    flattened = landed.reshape(-1, landed.shape[-1])
    return jnp.einsum("sp,sd->pd", select, flattened, preferred_element_type=F32)


def arrive(sent):
    landed = lax.all_to_all(sent, "exp", split_axis=0, concat_axis=0, tiled=True)
    return lax.all_gather(landed.reshape(-1, landed.shape[-1]), "rep", axis=0, tiled=True)


def depart(partial_value, experts, capacity):
    summed = lax.psum_scatter(partial_value.astype(BF16), "rep", scatter_dimension=0, tiled=True)
    return lax.all_to_all(
        summed.reshape(experts, capacity, summed.shape[-1]),
        "exp",
        split_axis=0,
        concat_axis=0,
        tiled=True,
    )


def local_general(tokens, gain, expert_ids, gates, w_in, w_out, cotangent):
    experts = lax.axis_size("exp")
    tok_count, features = tokens.shape
    capacity = max(2, 2 * tok_count // experts)
    values = tokens.astype(F32)
    normed, norm_back = jax.vjp(lambda entries: normalize(entries, gain), values)
    normed = normed.astype(BF16)
    select = slot_table(expert_ids, experts, capacity)
    x_sent = place_rows(select, jnp.repeat(normed, 2, axis=0), experts, capacity)
    scaled = (cotangent.astype(F32)[:, None, :] * gates[:, :, None]).astype(BF16)
    d_sent = place_rows(select, scaled.reshape(2 * tok_count, features), experts, capacity)
    w_first, w_second = w_in[0], w_out[0]
    in_rows = arrive(x_sent)
    preact = jnp.dot(in_rows, w_first, preferred_element_type=F32)
    activated, act_back = jax.vjp(activate, preact)
    hidden = activated.astype(BF16)
    y_back = depart(jnp.dot(hidden, w_second, preferred_element_type=F32), experts, capacity)
    grad_rows = arrive(d_sent)
    d_hidden = jnp.einsum("rd,fd->rf", grad_rows, w_second, preferred_element_type=F32)
    d_pre = act_back(d_hidden)[0].astype(BF16)
    grad_second = jnp.einsum("rf,rd->fd", hidden, grad_rows, preferred_element_type=F32)
    grad_first = jnp.einsum("rd,rf->df", in_rows, d_pre, preferred_element_type=F32)
    d_back = depart(
        jnp.einsum("rf,df->rd", d_pre, w_first, preferred_element_type=F32), experts, capacity
    )
    returned = take_rows(select, y_back).reshape(tok_count, 2, features)
    mixed = (values + jnp.sum(gates[:, :, None] * returned, axis=1)).astype(BF16)
    d_normed = jnp.sum(take_rows(select, d_back).reshape(tok_count, 2, features), axis=1)
    grad_tokens = (cotangent.astype(F32) + norm_back(d_normed)[0]).astype(BF16)
    return (mixed, grad_tokens, grad_first.astype(BF16)[None], grad_second.astype(BF16)[None])


def dot_nn(a, b):
    return jnp.dot(a, b, preferred_element_type=F32)


def dot_nt(a, b):
    return lax.dot_general(a, b, (((1,), (1,)), ((), ())), preferred_element_type=F32)


def dot_tn(a, b):
    return lax.dot_general(a, b, (((0,), (0,)), ((), ())), preferred_element_type=F32)


def slots_of(ids, me, experts, capacity):
    count = ids[0].shape[0]
    chips = experts // 2
    lanes = lax.broadcasted_iota(jnp.int32, (count, 128), 1)
    hit = [(i == lanes).astype(F32) for i in ids]
    row = lax.broadcasted_iota(jnp.int32, (count, count), 0)
    col = lax.broadcasted_iota(jnp.int32, (count, count), 1)
    before = dot_nn((col < row).astype(BF16), (hit[0] + hit[1]).astype(BF16))
    slots = []
    for k in range(2):
        rank = jnp.sum(before * hit[k], axis=1, keepdims=True).astype(jnp.int32)
        label = ids[k] ^ me
        block = (label & 1) * chips + (label >> 1)
        slots.append(jnp.where(rank < capacity, block * capacity + rank, -1))
    return slots


def row_stats(values):
    center = values - jnp.mean(values, axis=-1, keepdims=True)
    spread = jnp.mean(center * center, axis=-1, keepdims=True)
    return center, lax.rsqrt(spread + epsilon)


def column(row):
    size = row.shape[1]
    here = lax.broadcasted_iota(jnp.int32, (size, size), 0) == lax.broadcasted_iota(jnp.int32, (size, size), 1)
    return jnp.sum(jnp.where(here, row, 0.0), axis=1, keepdims=True)


def send_kernel(experts, capacity, me_ref, *refs):
    sources, (keep_ref, swap_ref, slot_ref, gate_ref) = refs[:5], refs[5:9]
    landing, sems = refs[9:14], refs[14]
    copies = [pltpu.make_async_copy(a, b, sems.at[i]) for i, (a, b) in enumerate(zip(sources, landing))]
    for c in copies:
        c.start()
    id_rows, gate_rows, tok_ref, gain_ref, cot_ref = landing
    count, features = tok_ref.shape
    half = experts // 2 * capacity
    copies[0].wait()
    ids = [column(id_rows[k : k + 1, :].astype(F32)).astype(jnp.int32) for k in range(2)]
    slots = slots_of(ids, me_ref[0], experts, capacity)
    lane = lax.broadcasted_iota(jnp.int32, (count, 2 * half), 1)
    picks = [(slots[k] == lane).astype(F32) for k in range(2)]
    second = lax.broadcasted_iota(jnp.int32, (count, 2), 1) == 1
    slot_ref[...] = jnp.where(second, slots[1], slots[0])
    copies[1].wait()
    gates = [column(gate_rows[k : k + 1, :]) for k in range(2)]
    gate_ref[...] = jnp.where(second, gates[1], gates[0])
    copies[2].wait()
    copies[3].wait()
    center, scale = row_stats(tok_ref[...].astype(F32))
    normed = (center * scale * gain_ref[...]).astype(BF16)
    copies[4].wait()
    cot = cot_ref[...].astype(F32)
    scaled = jnp.concatenate([(cot * g).astype(BF16) for g in gates], axis=0)
    pick_x = (picks[0] + picks[1]).astype(BF16)
    pick_d = jnp.concatenate([p.astype(BF16) for p in picks], axis=0)
    for part, out in ((1, swap_ref), (0, keep_ref)):
        at = slice(part * half, (part + 1) * half)
        out[:, :features] = dot_tn(pick_x[:, at], normed).astype(BF16)
        out[:, features:] = dot_tn(pick_d[:, at], scaled).astype(BF16)


def expert_kernel(pieces, form, *refs):
    parts, (w1_ref, w2_ref), outs = refs[:pieces], refs[pieces : pieces + 2], refs[pieces + 2 : -4]
    x_ref, d_ref, hid_ref, pre_ref = refs[-4:]
    count, width = parts[0].shape
    features = width // 2
    hidden_units = w1_ref.shape[1]
    tile = min(256, hidden_units)
    x_rows = jnp.concatenate([p[:, :features] for p in parts], axis=0)
    d_rows = jnp.concatenate([p[:, features:] for p in parts], axis=0)
    x_ref[...], d_ref[...] = x_rows, d_rows
    for j in range(0, hidden_units, tile):
        at = slice(j, j + tile)
        v = dot_nn(x_rows, w1_ref[:, at])
        dh = dot_nt(d_rows, w2_ref[at, :])
        v2 = v * v
        t = jnp.tanh(v * (ROOT_2_PI + (ROOT_2_PI * CUBIC) * v2))
        hid_ref[:, at] = (0.5 * v * (1.0 + t)).astype(BF16)
        slope = 0.5 * (1.0 + t) + 0.5 * v * (1.0 - t * t) * (ROOT_2_PI + (3.0 * ROOT_2_PI * CUBIC) * v2)
        pre_ref[:, at] = (dh * slope).astype(BF16)
    hid, pre = hid_ref[...], pre_ref[...]
    half = count // 2
    if form == 3:
        moves = (
            (0, 0, half, 0, 0),
            (1, 0, half, 1, 0),
            (3, 0, half, 1, half),
            (2, 0, half, 2, 0),
            (2, half, count, 3, 0),
            (3, half, count, 3, half),
            (1, half, count, 3, count),
            (0, half, count, 3, count + half),
        )
    elif form == 2:
        moves = (
            (0, 0, count, 0, 0),
            (1, 0, half, 1, 0),
            (3, 0, half, 1, half),
            (2, half, count, 2, 0),
            (3, half, count, 2, half),
            (2, 0, half, 3, 0),
            (1, half, count, 4, 0),
        )
    else:
        near, then = (2, 1) if form == 0 else (1, 2)
        moves = ((0, 0, count, 0, 0), (near, 0, count, 1, 0), (3, 0, count, 1, count), (then, 0, count, 2, 0))
    for j in range(0, features, tile):
        y = dot_nn(hid, w2_ref[:, j : j + tile]).astype(BF16)
        dx = dot_nt(pre, w1_ref[j : j + tile, :]).astype(BF16)
        for rep, low, high, out, to in moves:
            rows, there = slice(rep * count + low, rep * count + high), slice(to, to + high - low)
            outs[out][there, j : j + tile] = y[rows]
            outs[out][there, features + j : features + j + tile] = dx[rows]


def grad_kernel(chips, base, *refs):
    if base:
        refs = refs[1:]
    left, right, out_ref = refs[:chips], refs[chips : 2 * chips], refs[2 * chips]
    tile = out_ref.shape[0]
    at = pl.ds(pl.multiple_of((pl.program_id(0) + base) * tile, tile), tile)
    total = dot_tn(left[0][:, at], right[0][...])
    for k in range(1, chips):
        total = total + dot_tn(left[k][:, at], right[k][...])
    out_ref[...] = total.astype(BF16)


def last_kernel(capacity, chips, late, slot_ref, tok_ref, gain_ref, gate_ref, cot_ref, *refs):
    pieces, mixed_ref, grad_ref = refs[:-2], refs[-2], refs[-1]
    count, features = tok_ref.shape
    odd = [pieces[k][capacity:] for k in range(chips)]
    for i, k in enumerate(late):
        odd[k] = pieces[chips][i * capacity : (i + 1) * capacity]
    returned = jnp.concatenate([p[:capacity] for p in pieces[:chips]] + odd, axis=0)
    lane = lax.broadcasted_iota(jnp.int32, (count, returned.shape[0]), 1)
    picks = [(slot_ref[:, k : k + 1] == lane).astype(F32) for k in range(2)]
    values = tok_ref[...].astype(F32)
    total = None
    for k in range(2):
        term = gate_ref[:, k : k + 1] * dot_nn(picks[k].astype(BF16), returned[:, :features])
        total = term if total is None else total + term
    mixed_ref[...] = (values + total).astype(BF16)
    d_normed = dot_nn((picks[0] + picks[1]).astype(BF16), returned[:, features:])
    center, scale = row_stats(values)
    down = d_normed * gain_ref[...]
    along = jnp.sum(down * center, axis=-1, keepdims=True) * (1.0 / features)
    d_center = down * scale - center * (scale * scale * scale * along)
    d_values = d_center - jnp.mean(d_center, axis=-1, keepdims=True)
    grad_ref[...] = (cot_ref[...].astype(F32) + d_values).astype(BF16)


def vmem(array):
    return pltpu.with_memory_space_constraint(array, pltpu.VMEM)


def call(kernel, outs, args, limit=24, **kwargs):
    spec = pl.BlockSpec(memory_space=pltpu.VMEM)
    return pl.pallas_call(
        kernel,
        out_shape=tuple(pltpu.VMEM(s, d) for s, d in outs),
        in_specs=[spec] * len(args),
        out_specs=tuple(spec for _ in outs),
        compiler_params=pltpu.CompilerParams(vmem_limit_bytes=limit << 20),
        **kwargs,
    )(*[vmem(a) for a in args])


def flip(array, axis_name, mask):
    size = lax.axis_size(axis_name)
    return lax.ppermute(array, axis_name, [(i, i ^ mask) for i in range(size)])


def f32(array):
    return array.astype(F32)


def local(tokens, gain, expert_ids, gates, w_in, w_out, cotangent):
    return local_inner(tokens, gain, expert_ids, gates, w_in, w_out, cotangent)


def local_inner(tokens, gain, expert_ids, gates, w_in, w_out, cotangent):
    experts = lax.axis_size("exp")
    chips = experts // 2
    tok_count, features = tokens.shape
    capacity = max(2, 2 * tok_count // experts)
    me = lax.axis_index("exp").astype(jnp.int32).reshape(1)
    gain_row = gain.reshape(1, features)
    wide = 2 * features
    half = chips * capacity
    count = 2 * capacity
    spec = pl.BlockSpec(memory_space=pltpu.VMEM)
    there = [pltpu.with_memory_space_constraint(a, pltpu.HBM) for a in (expert_ids.T, gates.T, tokens, gain_row, cotangent)]
    keep, swap, slots, gate_columns = pl.pallas_call(
        functools.partial(send_kernel, experts, capacity),
        out_shape=(
            pltpu.VMEM((half, wide), BF16),
            pltpu.VMEM((half, wide), BF16),
            pltpu.VMEM((tok_count, 2), jnp.int32),
            pltpu.VMEM((tok_count, 2), F32),
        ),
        in_specs=[pl.BlockSpec(memory_space=pltpu.SMEM)] + [pl.BlockSpec(memory_space=pltpu.HBM)] * 5,
        out_specs=(spec,) * 4,
        scratch_shapes=[pltpu.VMEM(a.shape, a.dtype) for a in there] + [pltpu.SemaphoreType.DMA((5,))],
        compiler_params=pltpu.CompilerParams(vmem_limit_bytes=16 << 20),
        name="send",
    )(me, *there)
    swapped = flip(swap, "exp", 1)
    w_first, w_second = w_in[0], w_out[0]
    units = w_first.shape[1]
    landed = {}
    for k in range(chips):
        at = slice(k * capacity, (k + 1) * capacity)
        own = jnp.concatenate([keep[at], swapped[at]], axis=0)
        landed[k] = flip(own, "exp", 2 * k) if k else own
    rows, tall, parts = {}, {}, {}
    for k in range(chips):
        own = landed[k]
        by_x, by_y = flip(own, "rep", 1), flip(own, "rep", 2)
        if GATHER[k] == 0:
            far = (flip(by_y, "rep", 1),)
        elif GATHER[k] == 1:
            far = (flip(by_x, "rep", 2),)
        else:
            far = (flip(by_y[:capacity], "rep", 1), flip(by_x[capacity:], "rep", 2))
        rows[k] = (own, by_x, by_y, *far)
        if SCATTER[k] == 3:
            sizes = (capacity, count, capacity, 2 * count)
        else:
            sizes = (count, count, count, capacity, capacity) if SCATTER[k] == 2 else (count, 2 * count, count)
        *leaving, x_all, d_all, hid, pre = call(
            functools.partial(expert_kernel, len(rows[k]), SCATTER[k]),
            tuple(((n, wide), BF16) for n in sizes)
            + (((4 * count, features), BF16),) * 2
            + (((4 * count, units), BF16),) * 2,
            (*rows[k], w_first, w_second),
            cost_estimate=pl.CostEstimate(
                flops=8 * 4 * count * features * units, bytes_accessed=4 * features * units, transcendentals=0
            ),
        )
        tall[k], parts[k] = ((hid, d_all), (x_all, pre)), leaving
    back = {}
    for k in range(chips):
        if SCATTER[k] >= 2:
            if SCATTER[k] == 3:
                own, to_x, via_y, swap_k = parts[k]
                swap_k = flip(swap_k, "exp", 1)
                to_y = swap_k[:count]
                via_x = swap_k[count : count + capacity]
                own = jnp.concatenate([own, swap_k[count + capacity :]], axis=0)
            else:
                own, to_x, to_y, via_y, via_x = parts[k]
            got_x, got_y = flip(to_x, "rep", 1), flip(to_y, "rep", 2)
            sum_a = (f32(via_y) + f32(got_x[capacity:])).astype(BF16)
            sum_b = (f32(via_x) + f32(got_y[capacity:])).astype(BF16)
            last_a, last_b = flip(sum_a, "rep", 2), flip(sum_b, "rep", 1)
            near = jnp.concatenate([got_x[:capacity], got_y[:capacity]], axis=0)
            summed = (f32(own) + f32(near) + f32(jnp.concatenate([last_a, last_b], axis=0))).astype(BF16)
        else:
            own, near, then = parts[k]
            first, second = (2, 1) if SCATTER[k] == 0 else (1, 2)
            got = flip(near, "rep", first)
            last = flip((f32(then) + f32(got[count:])).astype(BF16), "rep", second)
            summed = (f32(own) + f32(got[:count]) + f32(last)).astype(BF16)
        back[k] = flip(summed, "exp", 2 * k) if k else summed
    grads = []
    for first in (False, True):
        args = [vmem(tall[k][first][i]) for i in range(2) for k in range(chips)]
        size = (features, units) if first else (units, features)
        tile = min(256, size[0])
        steps = size[0] // tile
        done = None
        for base in (0, steps // 2):
            done = pl.pallas_call(
                functools.partial(grad_kernel, chips, base),
                out_shape=jax.ShapeDtypeStruct(size, BF16),
                grid=(steps - base if base else steps // 2,),
                in_specs=([pl.BlockSpec(memory_space=pl.ANY)] if base else []) + [spec] * len(args),
                out_specs=pl.BlockSpec((tile, size[1]), lambda i, base=base: (i + base, 0)),
                input_output_aliases={0: 0} if base else {},
                compiler_params=pltpu.CompilerParams(vmem_limit_bytes=24 << 20),
                name="grad_in" if first else "grad_out",
                cost_estimate=pl.CostEstimate(
                    flops=chips * 4 * count * size[0] * size[1],
                    bytes_accessed=size[0] * size[1],
                    transcendentals=0,
                ),
            )(*([done] if base else []), *args)
        grads.append(done)
    late = [k for k in range(chips) if SCATTER[k] != 3]
    other = flip(jnp.concatenate([back[k][capacity:] for k in late], axis=0), "exp", 1) if late else None
    ready = [vmem(back[k]) for k in range(chips)]
    if late:
        ready.append(vmem(other))
    mixed, grad_tokens = pl.pallas_call(
        functools.partial(last_kernel, capacity, chips, late),
        out_shape=(jax.ShapeDtypeStruct((tok_count, features), BF16),) * 2,
        in_specs=[spec] * (5 + len(ready)),
        out_specs=(spec,) * 2,
        compiler_params=pltpu.CompilerParams(vmem_limit_bytes=24 << 20),
        name="last",
    )(
        vmem(slots),
        tokens,
        gain_row,
        vmem(gate_columns),
        cotangent,
        *ready,
    )
    return (mixed, grad_tokens, grads[1][None], grads[0][None])


def solution(mesh):
    rep, exp = mesh.shape["rep"], mesh.shape["exp"]

    def body(tokens, *rest):
        fits = rep == 4 and exp == 8 and (2 * tokens.shape[0] // exp) % 16 == 0
        return (local if fits else local_general)(tokens, *rest)

    return jax.shard_map(
        body,
        mesh=mesh,
        in_specs=(
            P(("rep", "exp"), None),
            P(),
            P(("rep", "exp"), None),
            P(("rep", "exp"), None),
            P("exp", None, "rep"),
            P("exp", "rep", None),
            P(("rep", "exp"), None),
        ),
        out_specs=(
            P(("rep", "exp"), None),
            P(("rep", "exp"), None),
            P("exp", None, "rep"),
            P("exp", "rep", None),
        ),
        check_vma=False,
    )
```
